32 devices in a mesh: band: 16 (over z, y, core), grid: 2 (over x).
Axes of the slice: x: 2, y: 2, z: 4, core: 2. Of those that a mesh axis runs over, the one named last changes fastest.
Arguments:
- orbitals: float32 [32, 48, 2304], P('band', 'grid'), may hold values from -6 to 6
- occupation: float32 [32], P('band'), may hold values from 0.2 to 1
Outputs:
- exchange: float32 [32, 48, 2304], P('band', 'grid')
The draws below stay inside these ranges and needn't reach their ends.
All inputs are finite; a program needn't handle non-finite values.
Results may differ from the reference program's by a relative error of at most 0.0003.
Values sent between devices are 32-bit elements; how exact they have to be, the bound alone decides.
A program may use at most 64 MiB of HBM per device.

```python
import jax
import jax.numpy as jnp
from jax import lax

GX = 48
GY = 48
GZ = 48
ORB_DEV = 2
STOPS = 3
ORBITALS = 32
N_BAND = 16


def block_levels(key, extent, cuts, least, high):
    def one(position, parts):
        draws = jax.random.uniform(jax.random.fold_in(jax.random.fold_in(key, 6), position), (parts,), jnp.float32, least / len(cuts), high / len(cuts))
        return jnp.repeat(jnp.exp(draws), extent[position] // parts).reshape((-1,) + (1,) * (len(extent) - position - 1))

    factor_of = one(*cuts[0])
    for cut in cuts[1:]:
        factor_of = factor_of * one(*cut)
    return factor_of


def normal_values(stream_key, extent, deviation, bound, cuts=(), kind=jnp.bfloat16):
    array = jax.random.normal(stream_key, extent, jnp.float32) * deviation
    if len(cuts) > 0:
        array = block_levels(stream_key, extent, cuts, -0.22, 0.18) * array
    return jnp.clip(array, min=-bound, max=bound).astype(kind)


def setup_inputs(seed: int = 0) -> dict:
    streams_of = jax.random.split(jax.random.key(seed), 3)
    orbitals = normal_values(streams_of[0], (ORBITALS, GX, GY * GZ), 1.0, 6.0, ((0, 16), (1, 2)), jnp.float32)
    occupation = jnp.clip(0.2 + 0.8 * jax.random.uniform(streams_of[1], (ORBITALS,), jnp.float32) ** block_levels(streams_of[1], (ORBITALS,), ((0, 16),), -0.2, 0.2), 0.2, 1.0)
    return dict(orbitals=orbitals, occupation=occupation)


def signed_square(length, count):
    index = jnp.arange(count, dtype=jnp.int32)
    signed = jnp.where(index <= length // 2, index, index - length)
    return (signed * signed).astype(jnp.float32)


def make_kernel():
    total = (signed_square(GX, GX)[:, None, None] + signed_square(GY, GY)[None, :, None]
             + signed_square(GZ, GZ // 2 + 1)[None, None, :])
    safe = jnp.where(total > 0, total, jnp.ones_like(total))
    return jnp.where(total > 0, (24.0 * 24.0 / jnp.pi) / safe, jnp.zeros_like(total))


def reference(orbitals, occupation):
    psi = orbitals.reshape(N_BAND, ORB_DEV, GX, GY, GZ)
    occ = occupation.reshape(N_BAND, ORB_DEV)
    kernel = make_kernel()

    def one_block(block):
        visit = lax.dynamic_index_in_dim(psi, block, 0, keepdims=False)
        total = jnp.zeros((ORB_DEV, GX, GY, GZ), jnp.float32)
        for stop in range(STOPS):
            other = ((block + stop) % N_BAND).astype(jnp.int32)
            own = lax.dynamic_index_in_dim(psi, other, 0, keepdims=False)
            weight = lax.dynamic_index_in_dim(occ, other, 0, keepdims=False)
            dens = own[:, None] * visit[None]
            spectrum = jnp.fft.rfftn(dens, axes=(2, 3, 4)) * kernel
            pot = jnp.fft.irfftn(spectrum, s=(GX, GY, GZ), axes=(2, 3, 4)).astype(jnp.float32)
            weighted = own * weight[:, None, None, None]
            total = total - 0.25 * jnp.einsum('ijxyz,ixyz->jxyz', pot, weighted,
                                              precision=lax.Precision.HIGHEST)
        return total

    out = lax.map(one_block, jnp.arange(N_BAND, dtype=jnp.int32))
    return out.reshape(ORBITALS, GX, GY * GZ).astype(jnp.float32)
```

```python
import jax
import jax.numpy as jnp
import numpy as np
from jax import lax
from jax.experimental import pallas as pl
from jax.experimental.pallas import tpu as pltpu
from jax.sharding import PartitionSpec as P

N = 48
HALF = N // 2
PLANE = N * N
COLS = PLANE // 2
STOPS = 3
PAD = 8
SIDE = 3 * HALF + PAD
MESH = pl.DeviceIdType.MESH
CUTS = [(0, 256), (256, 256), (512, 256), (768, 256), (1024, 128)]


def cas(product, length):
    angle = (product % length) * (2.0 * np.pi / length)
    return np.cos(angle) + np.sin(angle)


def tables():
    i, h = np.arange(N), np.arange(HALF)
    along_z = np.tile(cas(i[:, None] * i[None, :], N), (1, HALF))
    even = cas(2 * h[:, None] * h[None, :], N)
    odd = cas(h[:, None] * (2 * h[None, :] + 1), N)
    along_y = np.stack([np.repeat(m, N, axis=1) for m in (even, odd, odd.T)])
    square = np.where(i <= HALF, i, i - N).astype(np.float64) ** 2
    order = np.concatenate([i[0::2], i[1::2]])
    total = square[:, None, None] + square[order][None, :, None] + square[None, None, :]
    coulomb = np.where(total > 0, 24.0 * 24.0 / np.pi / np.where(total > 0, total, 1.0), 0.0)
    coulomb = coulomb.reshape(N, PLANE) * (-0.25 / N**3)
    along_x = cas(i[:, None] * i[None, :], N)
    x_high = along_x.astype(np.float32).astype(jnp.bfloat16)
    x_low = (along_x - x_high.astype(np.float64)).astype(np.float32).astype(jnp.bfloat16)
    there, back = [], []
    for place in range(2):
        halves = [slice(s * HALF, (s + 1) * HALF) for s in (place, 1 - place)]
        pad = np.zeros((N, PAD), x_high.dtype)
        there.append(
            np.concatenate(
                [b for s in halves for b in (x_high[:, s], x_high[:, s], x_low[:, s], pad)], axis=1
            )
        )
        high, low = (np.concatenate([m[s] for s in halves]) for m in (x_high, x_low))
        back.append(np.concatenate([high, high, low], axis=1))
    return (
        along_z.astype(np.float32),
        along_y.astype(np.float32),
        np.stack(there),
        np.stack(back),
        coulomb.astype(np.float32),
    )


def split(value):
    high = value.astype(jnp.bfloat16)
    return high, (value - high.astype(jnp.float32)).astype(jnp.bfloat16)


def split32(value):
    high = value.astype(jnp.bfloat16).astype(jnp.float32)
    return high, value - high


def dot(a, b):
    return jnp.dot(a, b, preferred_element_type=jnp.float32)


def kernel(
    occ_in, psi_in, z_in, y_in, there_in, back_in, coulomb_in,
    out, occ, psi, along_z, along_y, there, back, coulomb,
    buf, w_high, w_low, slabs, lhs, xrhs, acc, load, send, recv, out_send, out_recv,
):
    sources = (psi_in, z_in, y_in, there_in, back_in, coulomb_in)
    targets = (psi, along_z, along_y, there, back, coulomb)
    loads = [pltpu.make_async_copy(a, b, load.at[i]) for i, (a, b) in enumerate(zip(sources, targets))]
    weights = pltpu.make_async_copy(occ_in, occ, load.at[6])
    weights.start()
    for c in loads:
        c.start()
    band, grid = lax.axis_index("band"), lax.axis_index("grid")
    devices = lax.axis_size("band")
    left = {"band": lax.rem(band + devices - 1, devices), "grid": grid}
    right = {"band": lax.rem(band + 1, devices), "grid": grid}
    across = {"band": band, "grid": 1 - grid}
    odd = lax.rem(band, 2) == 1

    barrier = pltpu.get_barrier_semaphore()
    for device in (across, right):
        pl.semaphore_signal(barrier, inc=1, device_id=device, device_id_type=MESH)

    def root(k):
        return jnp.sqrt(jnp.full((1, 128), occ[k], jnp.float32))

    weights.wait()
    loads[0].wait()
    for k in range(2):
        factor = root(k)
        for start in range(0, PLANE, 128):
            at = slice(start, start + 128)
            buf[0, k, 0, :, at] = psi[k, :, at] * factor

    def copy(number, k, source, target, device):
        return pltpu.make_async_remote_copy(
            src_ref=buf.at[source[0], k, source[1]],
            dst_ref=buf.at[target[0], k, target[1]],
            send_sem=send.at[number, k],
            recv_sem=recv.at[target[0], target[1], k],
            device_id=device,
            device_id_type=MESH,
        )

    swap = [copy(0, k, (0, 0), (0, 1), across) for k in (1 - grid, grid)]
    own = [copy(1, k, (0, 0), (1, 0), left) for k in range(2)]
    own_on = [copy(2, k, (1, 0), (2, 0), left) for k in range(2)]
    other = [copy(3, k, (0, 1), (1, 1), left) for k in range(2)]
    other_on = [copy(4, k, (1, 1), (2, 1), left) for k in range(2)]
    other_swap = [copy(5, k, (2, 0), (2, 1), across) for k in range(2)]

    def start(copies):
        for c in copies:
            c.start()

    def arrived(copies):
        for c in copies:
            c.wait_recv()

    def build(m):
        @pl.loop(0, HALF)
        def _(y):
            rows = pl.ds(pl.multiple_of(y * N, 16), N)
            high, low = split(along_z[...] * along_y[m, pl.ds(y, 1), :])
            w_high[m, rows, :] = high
            w_low[m, rows, :] = low

    def forward(*parts):
        rows = N * len(parts)
        for first in range(0, COLS, 128):
            cols = [slice(s, s + 128) for s in (first, COLS + first)]
            low_y, high_y = (
                jnp.concatenate(
                    [
                        buf[0, grid, side, :, c] * buf[stop, k, side, :, c]
                        for stop, side in parts
                        for k in range(2)
                    ]
                )
                for c in cols
            )
            for parity, value in enumerate((low_y + high_y, low_y - high_y)):
                slabs[parity, :rows, cols[0]], slabs[parity, rows:, cols[0]] = split(value)
        for parity in range(2):
            for first, size in CUTS:
                cut = slice(first, first + size)
                both = dot(slabs[parity], w_high[parity, :, cut])
                value = both[:rows] + both[rows:] + dot(slabs[parity, :rows, :], w_low[parity, :, cut])
                high, low = split32(value)
                to = slice(parity * COLS + first, parity * COLS + first + size)
                pad = jnp.zeros((PAD, size), jnp.float32)
                for n, (stop, side) in enumerate(parts):
                    for k in range(2):
                        at = slice((2 * n + k) * HALF, (2 * n + k + 1) * HALF)
                        block = jnp.concatenate([high[at], low[at], high[at], pad])
                        xrhs[stop, k, side * SIDE : (side + 1) * SIDE, to] = block.astype(jnp.bfloat16)

    def finish(stops, hook=None):
        pairs = [(stop, k) for stop in stops for k in range(2)]
        rows = N * len(pairs)
        for first in range(0, PLANE, 256):
            at = slice(first, first + 256)
            for n, (stop, k) in enumerate(pairs):
                work = dot(there[grid], xrhs[stop, k, :, at]) * coulomb[:, at]
                high, low = split(work)
                work = dot(back[grid], jnp.concatenate([high, low, high]))
                high, low = split(work)
                lhs[n * N : (n + 1) * N, at] = high
                lhs[rows + n * N : rows + (n + 1) * N, at] = low

        def yz(which, parity, cut):
            half = slice(parity * COLS, (parity + 1) * COLS)
            both = dot(lhs[: 2 * rows, half], w_high[which, :, cut])
            return both[:rows] + both[rows:] + dot(lhs[:rows, half], w_low[which, :, cut])

        last = STOPS - 1 in stops
        scale = 1.0 / root(grid)[:, :1] if last else None
        sent = []
        for number, (first, size) in enumerate(CUTS):
            cols = [slice(s, s + size) for s in (first, COLS + first)]
            even, odd_y = yz(0, 0, cols[0]), yz(2, 1, cols[0])
            for at, value in zip(cols, (even + odd_y, even - odd_y)):
                for side in range(2):
                    part = slice(side * HALF, (side + 1) * HALF)
                    term = sum(
                        value[n * N + side * HALF : n * N + (side + 1) * HALF] * buf[stop, k, side, :, at]
                        for n, (stop, k) in enumerate(pairs)
                    )
                    if 0 not in stops:
                        term = term + acc[part, at]
                    if not last:
                        acc[part, at] = term
                    elif side == 0:
                        out[grid, :, at] = term * scale
                    else:
                        acc[part, at] = term * scale
                if last:
                    sent.append(
                        pltpu.make_async_remote_copy(
                            src_ref=acc.at[pl.ds(HALF, HALF), pl.ds(at.start, size)],
                            dst_ref=out.at[grid, :, pl.ds(at.start, size)],
                            send_sem=out_send.at[len(sent)],
                            recv_sem=out_recv.at[len(sent)],
                            device_id=across,
                            device_id_type=MESH,
                        )
                    )
                    sent[-1].start()
            if hook is not None and number == 2:
                hook()
        return sent

    def pass_other():
        arrived(other)

        @pl.when(odd)
        def _():
            start(other_on)

    pl.semaphore_wait(barrier, 2)
    start(swap)
    start(own)
    loads[1].wait()
    loads[2].wait()
    build(0)
    build(1)
    build(2)
    for c in loads[3:]:
        c.wait()
    arrived(own)
    start(own_on)
    forward((0, 0), (1, 0))
    arrived(swap)
    start(other)
    arrived(own_on)

    @pl.when(odd)
    def _():
        start(other_swap)

    forward((0, 1), (2, 0))
    finish([0], pass_other)
    arrived(other_on)
    forward((1, 1), (2, 1))
    sent = finish([1, 2])
    for c in swap + own + own_on + other:
        c.wait_send()

    @pl.when(odd)
    def _():
        for c in other_on + other_swap:
            c.wait_send()

    for c in sent:
        c.wait()


def per_device(orbitals, occupation):
    count, slab, plane = orbitals.shape
    vmem = pl.BlockSpec(memory_space=pltpu.VMEM)
    operands = [orbitals] + [jnp.asarray(t) for t in tables()]
    return pl.pallas_call(
        kernel,
        out_shape=jax.ShapeDtypeStruct((count, slab, plane), jnp.float32),
        in_specs=[pl.BlockSpec(memory_space=pltpu.HBM)] * 7,
        out_specs=vmem,
        scratch_shapes=[pltpu.SMEM((count,), jnp.float32)]
        + [pltpu.VMEM(t.shape, t.dtype) for t in operands]
        + [
            pltpu.VMEM((STOPS, count, 2, slab, plane), jnp.float32),
            pltpu.VMEM((3, COLS, COLS), jnp.bfloat16),
            pltpu.VMEM((3, COLS, COLS), jnp.bfloat16),
            pltpu.VMEM((2, 4 * N, COLS), jnp.bfloat16),
            pltpu.VMEM((8 * N, PLANE), jnp.bfloat16),
            pltpu.VMEM((STOPS, count, 2 * SIDE, plane), jnp.bfloat16),
            pltpu.VMEM((N, plane), jnp.float32),
            pltpu.SemaphoreType.DMA((7,)),
            pltpu.SemaphoreType.DMA((6, count)),
            pltpu.SemaphoreType.DMA((STOPS, 2, count)),
            pltpu.SemaphoreType.DMA((2 * len(CUTS),)),
            pltpu.SemaphoreType.DMA((2 * len(CUTS),)),
        ],
        compiler_params=pltpu.CompilerParams(
            vmem_limit_bytes=63 << 20, collective_id=0, has_side_effects=True
        ),
    )(occupation, *operands)


def solution(mesh):
    placed = (P("band", "grid", None), P("band"))
    return jax.shard_map(
        per_device, mesh=mesh, in_specs=placed, out_specs=P("band", "grid", None), check_vma=False
    )
```

```python
import jax
import jax.numpy as jnp
import numpy as np
from jax import lax
from jax.experimental import pallas as pl
from jax.experimental.pallas import tpu as pltpu
from jax.sharding import PartitionSpec as P

N = 48
HALF = N // 2
PLANE = N * N
COLS = PLANE // 2
STOPS = 3
PAD = 8
SIDE = 3 * HALF + PAD
MESH = pl.DeviceIdType.MESH
CUTS = [(0, 256), (256, 256), (512, 256), (768, 256), (1024, 128)]


def cas(product, length):
    angle = (product % length) * (2.0 * np.pi / length)
    return np.cos(angle) + np.sin(angle)


def tables():
    i, h = np.arange(N), np.arange(HALF)
    along_z = np.tile(cas(i[:, None] * i[None, :], N), (1, HALF))
    even = cas(2 * h[:, None] * h[None, :], N)
    odd = cas(h[:, None] * (2 * h[None, :] + 1), N)
    along_y = np.stack([np.repeat(m, N, axis=1) for m in (even, odd, odd.T)])
    square = np.where(i <= HALF, i, i - N).astype(np.float64) ** 2
    order = np.concatenate([i[0::2], i[1::2]])
    total = square[:, None, None] + square[order][None, :, None] + square[None, None, :]
    coulomb = np.where(total > 0, 24.0 * 24.0 / np.pi / np.where(total > 0, total, 1.0), 0.0)
    coulomb = coulomb.reshape(N, PLANE) * (-0.25 / N**3)
    along_x = cas(i[:, None] * i[None, :], N)
    x_high = along_x.astype(np.float32).astype(jnp.bfloat16)
    x_low = (along_x - x_high.astype(np.float64)).astype(np.float32).astype(jnp.bfloat16)
    there, back = [], []
    for place in range(2):
        halves = [slice(s * HALF, (s + 1) * HALF) for s in (place, 1 - place)]
        pad = np.zeros((N, PAD), x_high.dtype)
        there.append(
            np.concatenate(
                [b for s in halves for b in (x_high[:, s], x_high[:, s], x_low[:, s], pad)], axis=1
            )
        )
        high, low = (np.concatenate([m[s] for s in halves]) for m in (x_high, x_low))
        back.append(np.concatenate([high, high, low], axis=1))
    return (
        along_z.astype(np.float32),
        along_y.astype(np.float32),
        np.stack(there),
        np.stack(back),
        coulomb.astype(np.float32),
    )


def split(value):
    high = value.astype(jnp.bfloat16)
    return high, (value - high.astype(jnp.float32)).astype(jnp.bfloat16)


def split32(value):
    high = value.astype(jnp.bfloat16).astype(jnp.float32)
    return high, value - high


def dot(a, b):
    return jnp.dot(a, b, preferred_element_type=jnp.float32)


def kernel(
    occ_in, psi_in, z_in, y_in, there_in, back_in, coulomb_in,
    out, occ, psi, along_z, along_y, there, back, coulomb,
    buf, w_high, w_low, slabs, lhs, xrhs, mid, acc, load, send, recv, out_send, out_recv,
):
    sources = (psi_in, z_in, y_in, there_in, back_in, coulomb_in)
    targets = (psi, along_z, along_y, there, back, coulomb)
    loads = [pltpu.make_async_copy(a, b, load.at[i]) for i, (a, b) in enumerate(zip(sources, targets))]
    weights = pltpu.make_async_copy(occ_in, occ, load.at[6])
    weights.start()
    for c in loads:
        c.start()
    band, grid = lax.axis_index("band"), lax.axis_index("grid")
    devices = lax.axis_size("band")
    left = {"band": lax.rem(band + devices - 1, devices), "grid": grid}
    right = {"band": lax.rem(band + 1, devices), "grid": grid}
    across = {"band": band, "grid": 1 - grid}
    odd = lax.rem(band, 2) == 1

    barrier = pltpu.get_barrier_semaphore()
    for device in (across, right):
        pl.semaphore_signal(barrier, inc=1, device_id=device, device_id_type=MESH)

    def root(k):
        return jnp.sqrt(jnp.full((1, 128), occ[k], jnp.float32))

    weights.wait()
    loads[0].wait()
    for k in range(2):
        factor = root(k)
        for start in range(0, PLANE, 128):
            at = slice(start, start + 128)
            buf[0, k, 0, :, at] = psi[k, :, at] * factor

    def copy(number, k, source, target, device):
        return pltpu.make_async_remote_copy(
            src_ref=buf.at[source[0], k, source[1]],
            dst_ref=buf.at[target[0], k, target[1]],
            send_sem=send.at[number, k],
            recv_sem=recv.at[target[0], target[1], k],
            device_id=device,
            device_id_type=MESH,
        )

    swap = [copy(0, k, (0, 0), (0, 1), across) for k in (1 - grid, grid)]
    own = [copy(1, k, (0, 0), (1, 0), left) for k in range(2)]
    own_on = [copy(2, k, (1, 0), (2, 0), left) for k in range(2)]
    other = [copy(3, k, (0, 1), (1, 1), left) for k in range(2)]
    other_on = [copy(4, k, (1, 1), (2, 1), left) for k in range(2)]
    other_swap = [copy(5, k, (2, 0), (2, 1), across) for k in range(2)]

    def start(copies):
        for c in copies:
            c.start()

    def arrived(copies):
        for c in copies:
            c.wait_recv()

    def build(m):
        @pl.loop(0, HALF)
        def _(y):
            rows = pl.ds(pl.multiple_of(y * N, 16), N)
            high, low = split(along_z[...] * along_y[m, pl.ds(y, 1), :])
            w_high[m, rows, :] = high
            w_low[m, rows, :] = low

    def forward(*parts):
        rows = N * len(parts)
        for first in range(0, COLS, 128):
            cols = [slice(s, s + 128) for s in (first, COLS + first)]
            low_y, high_y = (
                jnp.concatenate(
                    [
                        buf[0, grid, side, :, c] * buf[stop, k, side, :, c]
                        for stop, side in parts
                        for k in range(2)
                    ]
                )
                for c in cols
            )
            for parity, value in enumerate((low_y + high_y, low_y - high_y)):
                slabs[parity, :rows, cols[0]], slabs[parity, rows:, cols[0]] = split(value)
        for parity in range(2):
            for first, size in CUTS:
                cut = slice(first, first + size)
                both = dot(slabs[parity], w_high[parity, :, cut])
                value = both[:rows] + both[rows:] + dot(slabs[parity, :rows, :], w_low[parity, :, cut])
                high, low = split32(value)
                to = slice(parity * COLS + first, parity * COLS + first + size)
                pad = jnp.zeros((PAD, size), jnp.float32)
                for n, (stop, side) in enumerate(parts):
                    for k in range(2):
                        at = slice((2 * n + k) * HALF, (2 * n + k + 1) * HALF)
                        block = jnp.concatenate([high[at], low[at], high[at], pad])
                        xrhs[stop, k, side * SIDE : (side + 1) * SIDE, to] = block.astype(jnp.bfloat16)

    def finish(stops, hook=None):
        pairs = [(stop, k) for stop in stops for k in range(2)]
        rows = N * len(pairs)
        for first in range(0, PLANE, 256):
            at = slice(first, first + 256)
            for n, (stop, k) in enumerate(pairs):
                work = dot(there[grid], xrhs[stop, k, :, at]) * coulomb[:, at]
                high, low = split(work)
                mid[n, :, at] = jnp.concatenate([high, low, high])
        for first in range(0, PLANE, 256):
            at = slice(first, first + 256)
            for n, (stop, k) in enumerate(pairs):
                work = dot(back[grid], mid[n, :, at])
                high, low = split(work)
                lhs[n * N : (n + 1) * N, at] = high
                lhs[rows + n * N : rows + (n + 1) * N, at] = low

        def yz(which, parity, cut):
            half = slice(parity * COLS, (parity + 1) * COLS)
            both = dot(lhs[: 2 * rows, half], w_high[which, :, cut])
            return both[:rows] + both[rows:] + dot(lhs[:rows, half], w_low[which, :, cut])

        last = STOPS - 1 in stops
        scale = 1.0 / root(grid)[:, :1] if last else None
        sent = []
        for number, (first, size) in enumerate(CUTS):
            cols = [slice(s, s + size) for s in (first, COLS + first)]
            even, odd_y = yz(0, 0, cols[0]), yz(2, 1, cols[0])
            for at, value in zip(cols, (even + odd_y, even - odd_y)):
                for side in range(2):
                    part = slice(side * HALF, (side + 1) * HALF)
                    term = sum(
                        value[n * N + side * HALF : n * N + (side + 1) * HALF] * buf[stop, k, side, :, at]
                        for n, (stop, k) in enumerate(pairs)
                    )
                    if 0 not in stops:
                        term = term + acc[part, at]
                    if not last:
                        acc[part, at] = term
                    elif side == 0:
                        out[grid, :, at] = term * scale
                    else:
                        acc[part, at] = term * scale
                if last:
                    sent.append(
                        pltpu.make_async_remote_copy(
                            src_ref=acc.at[pl.ds(HALF, HALF), pl.ds(at.start, size)],
                            dst_ref=out.at[grid, :, pl.ds(at.start, size)],
                            send_sem=out_send.at[len(sent)],
                            recv_sem=out_recv.at[len(sent)],
                            device_id=across,
                            device_id_type=MESH,
                        )
                    )
                    sent[-1].start()
            if hook is not None and number == 2:
                hook()
        return sent

    def pass_other():
        arrived(other)

        @pl.when(odd)
        def _():
            start(other_on)

    pl.semaphore_wait(barrier, 2)
    start(swap)
    start(own)
    loads[1].wait()
    loads[2].wait()
    build(0)
    build(1)
    build(2)
    for c in loads[3:]:
        c.wait()
    arrived(own)
    start(own_on)
    forward((0, 0), (1, 0))
    arrived(swap)
    start(other)
    arrived(own_on)

    @pl.when(odd)
    def _():
        start(other_swap)

    forward((0, 1), (2, 0))
    finish([0], pass_other)
    arrived(other_on)
    forward((1, 1), (2, 1))
    sent = finish([1, 2])
    for c in swap + own + own_on + other:
        c.wait_send()

    @pl.when(odd)
    def _():
        for c in other_on + other_swap:
            c.wait_send()

    for c in sent:
        c.wait()


def per_device(orbitals, occupation):
    count, slab, plane = orbitals.shape
    vmem = pl.BlockSpec(memory_space=pltpu.VMEM)
    operands = [orbitals] + [jnp.asarray(t) for t in tables()]
    return pl.pallas_call(
        kernel,
        out_shape=jax.ShapeDtypeStruct((count, slab, plane), jnp.float32),
        in_specs=[pl.BlockSpec(memory_space=pltpu.HBM)] * 7,
        out_specs=vmem,
        scratch_shapes=[pltpu.SMEM((count,), jnp.float32)]
        + [pltpu.VMEM(t.shape, t.dtype) for t in operands]
        + [
            pltpu.VMEM((STOPS, count, 2, slab, plane), jnp.float32),
            pltpu.VMEM((3, COLS, COLS), jnp.bfloat16),
            pltpu.VMEM((3, COLS, COLS), jnp.bfloat16),
            pltpu.VMEM((2, 4 * N, COLS), jnp.bfloat16),
            pltpu.VMEM((8 * N, PLANE), jnp.bfloat16),
            pltpu.VMEM((STOPS, count, 2 * SIDE, plane), jnp.bfloat16),
            pltpu.VMEM((4, 3 * N, plane), jnp.bfloat16),
            pltpu.VMEM((N, plane), jnp.float32),
            pltpu.SemaphoreType.DMA((7,)),
            pltpu.SemaphoreType.DMA((6, count)),
            pltpu.SemaphoreType.DMA((STOPS, 2, count)),
            pltpu.SemaphoreType.DMA((2 * len(CUTS),)),
            pltpu.SemaphoreType.DMA((2 * len(CUTS),)),
        ],
        compiler_params=pltpu.CompilerParams(
            vmem_limit_bytes=63 << 20, collective_id=0, has_side_effects=True
        ),
    )(occupation, *operands)


def solution(mesh):
    placed = (P("band", "grid", None), P("band"))
    return jax.shard_map(
        per_device, mesh=mesh, in_specs=placed, out_specs=P("band", "grid", None), check_vma=False
    )
```

```python
import jax
import jax.numpy as jnp
import numpy as np
from jax import lax
from jax.experimental import pallas as pl
from jax.experimental.pallas import tpu as pltpu
from jax.sharding import PartitionSpec as P

N = 48
HALF = N // 2
PLANE = N * N
BLOCK = 8 * N
WIDE = 2 * BLOCK
PAD = 8
SIDE = 3 * HALF + PAD
PAIRS = 6
ROWS = PAIRS * HALF
STRIP = 8
STRIPS = HALF // STRIP
LATE = (2, 3, 4, 5)
MESH = pl.DeviceIdType.MESH


def cas(product, length):
    angle = (product % length) * (2.0 * np.pi / length)
    return np.cos(angle) + np.sin(angle)


def tables():
    i = np.arange(N)
    classes = [i[i % 3 == 0], i[(i % 6 == 2) | (i % 6 == 4)], i[(i % 6 == 1) | (i % 6 == 5)]]
    along_z = np.tile(cas(i[:, None] * i[None, :], N), (1, 16))
    ways = [cas(np.arange(16)[:, None] * k[None, :], N) for k in classes]
    along_y = np.stack([np.repeat(m, N, axis=1) for m in (*ways, ways[1].T, ways[2].T)])
    square = np.where(i <= HALF, i, i - N).astype(np.float64) ** 2
    order = np.concatenate(classes)
    total = square[:, None, None] + square[order][None, :, None] + square[None, None, :]
    coulomb = np.where(total > 0, 24.0 * 24.0 / np.pi / np.where(total > 0, total, 1.0), 0.0)
    coulomb = coulomb.reshape(N, PLANE) * (-0.25 / N**3)
    along_x = cas(i[:, None] * i[None, :], N)
    x_high = along_x.astype(np.float32).astype(jnp.bfloat16)
    x_low = (along_x - x_high.astype(np.float64)).astype(np.float32).astype(jnp.bfloat16)
    there, back = [], []
    for place in range(2):
        halves = [slice(s * HALF, (s + 1) * HALF) for s in (place, 1 - place)]
        pad = np.zeros((N, PAD), x_high.dtype)
        there.append(
            np.concatenate(
                [b for s in halves for b in (x_high[:, s], x_high[:, s], x_low[:, s], pad)], axis=1
            )
        )
        high, low = (np.concatenate([m[s] for s in halves]) for m in (x_high, x_low))
        back.append(np.concatenate([high, high, low], axis=1))
    return (
        along_z.astype(np.float32),
        along_y.astype(np.float32),
        np.stack(there),
        np.stack(back),
        coulomb.astype(np.float32),
    )


def split(value):
    high = value.astype(jnp.bfloat16)
    return high, (value - high.astype(jnp.float32)).astype(jnp.bfloat16)


def split32(value):
    high = value.astype(jnp.bfloat16).astype(jnp.float32)
    return high, value - high


def dot(a, b):
    return jnp.dot(a, b, preferred_element_type=jnp.float32)


def kernel(
    occ_in, psi_in, z_in, y_in, there_in, back_in, coulomb_in,
    out, occ, psi, along_z, along_y, there, back, coulomb,
    buf, w_high, w_low, slabs, xrhs, mid, lhs, pots, acc, load, send, recv, out_send, out_recv,
):
    weights = pltpu.make_async_copy(occ_in, occ, load.at[6])
    weights.start()
    sources = (psi_in, z_in, y_in, there_in, back_in, coulomb_in)
    targets = (psi, along_z, along_y, there, back, coulomb)
    loads = [pltpu.make_async_copy(a, b, load.at[i]) for i, (a, b) in enumerate(zip(sources, targets))]
    for c in loads:
        c.start()
    band, grid = lax.axis_index("band"), lax.axis_index("grid")
    devices = lax.axis_size("band")
    left = {"band": lax.rem(band + devices - 1, devices), "grid": grid}
    right = {"band": lax.rem(band + 1, devices), "grid": grid}
    across = {"band": band, "grid": 1 - grid}
    odd = lax.rem(band, 2) == 1

    barrier = pltpu.get_barrier_semaphore()
    for device in (across, right):
        pl.semaphore_signal(barrier, inc=1, device_id=device, device_id_type=MESH)

    def root(k):
        return jnp.sqrt(jnp.full((1, 128), occ[k], jnp.float32))

    weights.wait()
    loads[0].wait()
    for k in range(2):
        factor = root(k)
        for start in range(0, PLANE, 128):
            at = slice(start, start + 128)
            buf[0, k, 0, :, at] = psi[k, :, at] * factor

    def copy(number, k, source, target, device):
        return pltpu.make_async_remote_copy(
            src_ref=buf.at[source[0], k, source[1]],
            dst_ref=buf.at[target[0], k, target[1]],
            send_sem=send.at[number, k],
            recv_sem=recv.at[target[0], target[1], k],
            device_id=device,
            device_id_type=MESH,
        )

    swap = [copy(0, k, (0, 0), (0, 1), across) for k in range(2)]
    own = [copy(1, k, (0, 0), (1, 0), left) for k in range(2)]
    own_on = [copy(2, k, (1, 0), (2, 0), left) for k in range(2)]
    other = [copy(3, k, (0, 1), (1, 1), left) for k in range(2)]
    other_on = [copy(4, k, (1, 1), (2, 1), left) for k in range(2)]
    other_swap = [copy(5, k, (2, 0), (2, 1), across) for k in range(2)]

    def start(copies):
        for c in copies:
            c.start()

    def arrived(copies):
        for c in copies:
            c.wait_recv()

    def build(m):
        @pl.loop(0, 16)
        def _(y):
            rows = pl.ds(pl.multiple_of(y * N, 16), N)
            high, low = split(along_z[...] * along_y[m, pl.ds(y, 1), :])
            w_high[m, rows, :] = high
            w_low[m, rows, :] = low

    def products(*parts):
        rows = N * len(parts)
        for start in range(0, BLOCK, 128):
            cols = [slice(BLOCK * y + start, BLOCK * y + start + 128) for y in range(6)]
            for n, (stop, side) in enumerate(parts):
                to_rows = slice(n * N, (n + 1) * N)
                lows = slice(rows + n * N, rows + (n + 1) * N)
                a = [
                    jnp.concatenate([buf[0, grid, side, :, c] * buf[stop, k, side, :, c] for k in range(2)])
                    for c in cols
                ]
                plus = [a[y] + a[y + 3] for y in range(3)]
                minus = [a[y] - a[y + 3] for y in range(3)]
                sums = (
                    (a[0] + a[2] + a[4], a[1] + a[3] + a[5]),
                    (plus[0] - plus[2], plus[1] - plus[2]),
                    (minus[0] - minus[2], minus[1] + minus[2]),
                )
                for m, pair in enumerate(sums):
                    for y, value in enumerate(pair):
                        to = slice(y * BLOCK + start, y * BLOCK + start + 128)
                        slabs[m, to_rows, to], slabs[m, lows, to] = split(value)
    def forward_cut(number, parts):
        rows = N * len(parts)
        pad = jnp.zeros((PAD, 256), jnp.float32)
        m, cut = number // 3, slice(number % 3 * 256, number % 3 * 256 + 256)
        both = dot(slabs[m, : 2 * rows], w_high[m, :, cut])
        value = both[:rows] + both[rows:] + dot(slabs[m, :rows, :], w_low[m, :, cut])
        high, low = split32(value)
        to = slice(number * 256, number * 256 + 256)
        for n, (stop, side) in enumerate(parts):
            for k in range(2):
                at = slice((2 * n + k) * HALF, (2 * n + k + 1) * HALF)
                block = jnp.concatenate([high[at], low[at], high[at], pad])
                xrhs[2 * stop + k, side * SIDE : (side + 1) * SIDE, to] = block.astype(jnp.bfloat16)

    def there_cut(number, pairs):
        at = slice(number * 256, number * 256 + 256)
        for n in pairs:
            high, low = split(dot(there[grid], xrhs[n, :, at]) * coulomb[:, at])
            mid[n, :, at] = jnp.concatenate([high, low, high])

    def back_cut(number, pairs):
        at = slice(number * 256, number * 256 + 256)
        for n in pairs[::2]:
            one, two = dot(back[grid], mid[n, :, at]), dot(back[grid], mid[n + 1, :, at])
            for strip in range(2 * STRIPS):
                rows = slice(strip * STRIP, (strip + 1) * STRIP)
                high, low = split(jnp.concatenate([one[rows], two[rows]]))
                to = slice(n * STRIP, (n + 2) * STRIP)
                lhs[0, strip, to, at] = high
                lhs[1, strip, to, at] = low

    def turn_cut(number, strips, pairs):
        some = slice(pairs[0] * STRIP, (pairs[-1] + 1) * STRIP)
        rows = len(strips) * len(pairs) * STRIP
        m, cut = number // 3, slice(number % 3 * 256, number % 3 * 256 + 256)
        way = m + 2 if m else 0
        wide = slice(m * WIDE, (m + 1) * WIDE)
        high = jnp.concatenate([lhs[0, s, some, wide] for s in strips])
        low = jnp.concatenate([lhs[1, s, some, wide] for s in strips])
        both = dot(jnp.concatenate([high, low]), w_high[way, :, cut])
        pots[m, :rows, cut] = both[:rows] + both[rows:] + dot(high, w_low[way, :, cut])

    def forward(*parts):
        products(*parts)
        for number in range(9):
            forward_cut(number, parts)

    def chain(parts, pairs, strips):
        if parts:
            products(*parts)
        for step in range(14):
            if parts and step < 9:
                forward_cut(step, parts)
            if 0 <= step - 1 < 9:
                there_cut(step - 1, pairs)
            if 0 <= step - 2 < 9:
                back_cut(step - 2, pairs)
            if 0 <= step - 5:
                turn_cut(step - 5, strips, pairs)

    def weigh(number, side, strip, pairs, start, sums):
        at = slice(strip * STRIP, (strip + 1) * STRIP)
        for n in pairs:
            row = (number * len(pairs) + n - pairs[0]) * STRIP
            p, f, h = (
                [pots[m, row : row + STRIP, BLOCK * y + start : BLOCK * y + start + 128] for y in range(2)]
                for m in range(3)
            )
            f.append(-(f[0] + f[1]))
            h.append(h[1] - h[0])
            for y in range(6):
                value = p[y % 2] + f[y % 3]
                value = value + h[y] if y < 3 else value - h[y - 3]
                c = slice(BLOCK * y + start, BLOCK * y + start + 128)
                term = value * buf[n // 2, n % 2, side, at, c]
                sums[y] = term if sums[y] is None else sums[y] + term
        return sums

    def early():
        for number in range(2 * STRIPS):
            side, strip = divmod(number, STRIPS)
            for start in range(0, BLOCK, 128):
                sums = weigh(number, side, strip, (0, 1), start, [None] * 6)
                for y in range(6):
                    c = slice(BLOCK * y + start, BLOCK * y + start + 128)
                    acc[side, strip * STRIP : (strip + 1) * STRIP, c] = sums[y]

    def backward(side):
        if side == 0:
            for number in range(9):
                turn_cut(number, range(STRIPS), LATE)
        copies = []
        scale = 1.0 / root(grid)
        for strip in range(STRIPS):
            at = slice(strip * STRIP, (strip + 1) * STRIP)
            for start in range(0, BLOCK, 128):
                cols = [slice(BLOCK * y + start, BLOCK * y + start + 128) for y in range(6)]
                sums = weigh(strip, side, strip, LATE, start, [acc[side, at, c] for c in cols])
                for value, c in zip(sums, cols):
                    if side == 0:
                        out[grid, at, c] = value * scale
                    else:
                        acc[1, at, c] = value * scale
            if side == 1:
                rows = pl.ds(strip * STRIP, STRIP)
                copies.append(
                    pltpu.make_async_remote_copy(
                        src_ref=acc.at[1, rows],
                        dst_ref=out.at[grid, rows],
                        send_sem=out_send.at[strip],
                        recv_sem=out_recv.at[strip],
                        device_id=across,
                        device_id_type=MESH,
                    )
                )
                copies[-1].start()
        return copies

    even = jnp.logical_not(odd)

    pl.semaphore_wait(barrier, 2)
    start(own)

    @pl.when(even)
    def _():
        start(swap)

    loads[1].wait()
    loads[2].wait()
    for m in range(5):
        build(m)

    @pl.when(even)
    def _():
        for k in range(2):
            own[k].wait_recv()
            own_on[k].start()

    for k in range(2):
        @pl.when(even)
        def _():
            swap[k].wait_recv()
            other[k].start()

        @pl.when(odd)
        def _():
            own[k].wait_recv()
            swap[k].start()
            own_on[k].start()

    for c in loads[3:]:
        c.wait()
    forward((0, 0), (1, 0))

    for k in range(2):
        @pl.when(odd)
        def _():
            swap[k].wait_recv()
            other[k].start()

        own_on[k].wait_recv()

        @pl.when(odd)
        def _():
            other_swap[k].start()

    forward((0, 1), (2, 0))

    def pass_on(k):
        @pl.when(odd)
        def _():
            other[k].wait_recv()
            other_on[k].start()

    pass_on(0)
    chain((), (0, 1), range(2 * STRIPS))
    early()
    pass_on(1)

    @pl.when(even)
    def _():
        arrived(other)

    arrived(other_on)
    chain(((1, 1), (2, 1)), LATE, range(STRIPS, 2 * STRIPS))
    sent = backward(1)
    backward(0)
    for c in swap + own + own_on + other:
        c.wait_send()

    @pl.when(odd)
    def _():
        for c in other_on + other_swap:
            c.wait_send()

    for c in sent:
        c.wait()


def per_device(orbitals, occupation):
    count, slab, plane = orbitals.shape
    operands = [orbitals] + [jnp.asarray(t) for t in tables()]
    return pl.pallas_call(
        kernel,
        out_shape=jax.ShapeDtypeStruct((count, slab, plane), jnp.float32),
        in_specs=[pl.BlockSpec(memory_space=pltpu.HBM)] * 7,
        out_specs=pl.BlockSpec(memory_space=pltpu.VMEM),
        scratch_shapes=[pltpu.SMEM((count,), jnp.float32)]
        + [pltpu.VMEM(t.shape, t.dtype) for t in operands]
        + [
            pltpu.VMEM((3, count, 2, slab, plane), jnp.float32),
            pltpu.VMEM((5, WIDE, WIDE), jnp.bfloat16),
            pltpu.VMEM((5, WIDE, WIDE), jnp.bfloat16),
            pltpu.VMEM((3, 4 * N, WIDE), jnp.bfloat16),
            pltpu.VMEM((PAIRS, 2 * SIDE, plane), jnp.bfloat16),
            pltpu.VMEM((PAIRS, 3 * N, plane), jnp.bfloat16),
            pltpu.VMEM((2, 2 * STRIPS, PAIRS * STRIP, plane), jnp.bfloat16),
            pltpu.VMEM((3, 2 * ROWS // 3, WIDE), jnp.float32),
            pltpu.VMEM((2, slab, plane), jnp.float32),
            pltpu.SemaphoreType.DMA((7,)),
            pltpu.SemaphoreType.DMA((6, count)),
            pltpu.SemaphoreType.DMA((3, 2, count)),
            pltpu.SemaphoreType.DMA((STRIPS,)),
            pltpu.SemaphoreType.DMA((STRIPS,)),
        ],
        compiler_params=pltpu.CompilerParams(
            vmem_limit_bytes=63 << 20, collective_id=0, has_side_effects=True
        ),
    )(occupation, *operands)


def solution(mesh):
    placed = (P("band", "grid", None), P("band"))
    return jax.shard_map(
        per_device, mesh=mesh, in_specs=placed, out_specs=P("band", "grid", None), check_vma=False
    )
```

```python
import jax
import jax.numpy as jnp
import numpy as np
from jax import lax
from jax.experimental import pallas as pl
from jax.experimental.pallas import tpu as pltpu
from jax.sharding import PartitionSpec as P

N = 48
HALF = N // 2
PLANE = N * N
BLOCK = 8 * N
WIDE = 2 * BLOCK
PAD = 8
SIDE = 3 * HALF + PAD
PAIRS = 6
ROWS = PAIRS * HALF
STRIP = 8
STRIPS = HALF // STRIP
LATE = (2, 3, 4, 5)
MESH = pl.DeviceIdType.MESH


def cas(product, length):
    angle = (product % length) * (2.0 * np.pi / length)
    return np.cos(angle) + np.sin(angle)


def tables():
    i = np.arange(N)
    classes = [i[i % 3 == 0], i[(i % 6 == 2) | (i % 6 == 4)], i[(i % 6 == 1) | (i % 6 == 5)]]
    along_z = np.tile(cas(i[:, None] * i[None, :], N), (1, 16))
    ways = [cas(np.arange(16)[:, None] * k[None, :], N) for k in classes]
    along_y = np.stack([np.repeat(m, N, axis=1) for m in (*ways, ways[1].T, ways[2].T)])
    square = np.where(i <= HALF, i, i - N).astype(np.float64) ** 2
    order = np.concatenate(classes)
    total = square[:, None, None] + square[order][None, :, None] + square[None, None, :]
    coulomb = np.where(total > 0, 24.0 * 24.0 / np.pi / np.where(total > 0, total, 1.0), 0.0)
    coulomb = coulomb.reshape(N, PLANE) * (-0.25 / N**3)
    along_x = cas(i[:, None] * i[None, :], N)
    x_high = along_x.astype(np.float32).astype(jnp.bfloat16)
    x_low = (along_x - x_high.astype(np.float64)).astype(np.float32).astype(jnp.bfloat16)
    there, back = [], []
    for place in range(2):
        halves = [slice(s * HALF, (s + 1) * HALF) for s in (place, 1 - place)]
        pad = np.zeros((N, PAD), x_high.dtype)
        there.append(
            np.concatenate(
                [b for s in halves for b in (x_high[:, s], x_high[:, s], x_low[:, s], pad)], axis=1
            )
        )
        high, low = (np.concatenate([m[s] for s in halves]) for m in (x_high, x_low))
        back.append(np.concatenate([high, high, low], axis=1))
    return (
        along_z.astype(np.float32),
        along_y.astype(np.float32),
        np.stack(there),
        np.stack(back),
        coulomb.astype(np.float32),
    )


def split(value):
    high = value.astype(jnp.bfloat16)
    return high, (value - high.astype(jnp.float32)).astype(jnp.bfloat16)


def split32(value):
    high = value.astype(jnp.bfloat16).astype(jnp.float32)
    return high, value - high


def dot(a, b):
    return jnp.dot(a, b, preferred_element_type=jnp.float32)


def kernel(
    occ_in, psi_in, z_in, y_in, there_in, back_in, coulomb_in,
    out, occ, psi, along_z, along_y, there, back, coulomb,
    buf, w_high, w_low, slabs, xrhs, mid, lhs, pots, acc, load, send, recv, out_send, out_recv, keep,
):
    weights = pltpu.make_async_copy(occ_in, occ, load.at[6])
    weights.start()
    sources = (psi_in, z_in, y_in, there_in, back_in, coulomb_in)
    targets = (psi, along_z, along_y, there, back, coulomb)
    loads = [pltpu.make_async_copy(a, b, load.at[i]) for i, (a, b) in enumerate(zip(sources, targets))]
    for c in loads:
        c.start()
    band, grid = lax.axis_index("band"), lax.axis_index("grid")
    devices = lax.axis_size("band")
    left = {"band": lax.rem(band + devices - 1, devices), "grid": grid}
    right = {"band": lax.rem(band + 1, devices), "grid": grid}
    across = {"band": band, "grid": 1 - grid}
    odd = lax.rem(band, 2) == 1

    barrier = pltpu.get_barrier_semaphore()
    for device in (across, right):
        pl.semaphore_signal(barrier, inc=1, device_id=device, device_id_type=MESH)

    def root(k):
        return jnp.sqrt(jnp.full((1, 128), occ[k], jnp.float32))

    weights.wait()
    loads[0].wait()
    for k in range(2):
        factor = root(k)
        for start in range(0, PLANE, 128):
            at = slice(start, start + 128)
            buf[0, k, 0, :, at] = psi[k, :, at] * factor

    def copy(number, k, source, target, device):
        return pltpu.make_async_remote_copy(
            src_ref=buf.at[source[0], k, source[1]],
            dst_ref=buf.at[target[0], k, target[1]],
            send_sem=send.at[number, k],
            recv_sem=recv.at[target[0], target[1], k],
            device_id=device,
            device_id_type=MESH,
        )

    swap = [copy(0, k, (0, 0), (0, 1), across) for k in range(2)]
    own = [copy(1, k, (0, 0), (1, 0), left) for k in range(2)]
    own_on = [copy(2, k, (1, 0), (2, 0), left) for k in range(2)]
    other = [copy(3, k, (0, 1), (1, 1), left) for k in range(2)]
    other_on = [copy(4, k, (1, 1), (2, 1), left) for k in range(2)]
    other_swap = [copy(5, k, (2, 0), (2, 1), across) for k in range(2)]

    def start(copies):
        for c in copies:
            c.start()

    def arrived(copies):
        for c in copies:
            c.wait_recv()

    def build(m):
        @pl.loop(0, 16)
        def _(y):
            rows = pl.ds(pl.multiple_of(y * N, 16), N)
            high, low = split(along_z[...] * along_y[m, pl.ds(y, 1), :])
            w_high[m, rows, :] = high
            w_low[m, rows, :] = low

    def products(*parts):
        rows = N * len(parts)
        for start in range(0, BLOCK, 128):
            cols = [slice(BLOCK * y + start, BLOCK * y + start + 128) for y in range(6)]
            for n, (stop, side) in enumerate(parts):
                to_rows = slice(n * N, (n + 1) * N)
                lows = slice(rows + n * N, rows + (n + 1) * N)
                a = [
                    jnp.concatenate([buf[0, grid, side, :, c] * buf[stop, k, side, :, c] for k in range(2)])
                    for c in cols
                ]
                plus = [a[y] + a[y + 3] for y in range(3)]
                minus = [a[y] - a[y + 3] for y in range(3)]
                sums = (
                    (a[0] + a[2] + a[4], a[1] + a[3] + a[5]),
                    (plus[0] - plus[2], plus[1] - plus[2]),
                    (minus[0] - minus[2], minus[1] + minus[2]),
                )
                for m, pair in enumerate(sums):
                    for y, value in enumerate(pair):
                        to = slice(y * BLOCK + start, y * BLOCK + start + 128)
                        slabs[m, to_rows, to], slabs[m, lows, to] = split(value)
    def forward_cut(number, parts):
        rows = N * len(parts)
        pad = jnp.zeros((PAD, 256), jnp.float32)
        m, cut = number // 3, slice(number % 3 * 256, number % 3 * 256 + 256)
        both = dot(slabs[m, : 2 * rows], w_high[m, :, cut])
        value = both[:rows] + both[rows:] + dot(slabs[m, :rows, :], w_low[m, :, cut])
        high, low = split32(value)
        to = slice(number * 256, number * 256 + 256)
        for n, (stop, side) in enumerate(parts):
            for k in range(2):
                at = slice((2 * n + k) * HALF, (2 * n + k + 1) * HALF)
                block = jnp.concatenate([high[at], low[at], high[at], pad])
                xrhs[2 * stop + k, side * SIDE : (side + 1) * SIDE, to] = block.astype(jnp.bfloat16)

    def there_cut(number, pairs):
        at = slice(number * 256, number * 256 + 256)
        for n in pairs:
            high, low = split(dot(there[grid], xrhs[n, :, at]) * coulomb[:, at])
            mid[n, :, at] = jnp.concatenate([high, low, high])

    def back_cut(number, pairs):
        at = slice(number * 256, number * 256 + 256)
        for n in pairs[::2]:
            one, two = dot(back[grid], mid[n, :, at]), dot(back[grid], mid[n + 1, :, at])
            for strip in range(2 * STRIPS):
                rows = slice(strip * STRIP, (strip + 1) * STRIP)
                high, low = split(jnp.concatenate([one[rows], two[rows]]))
                to = slice(n * STRIP, (n + 2) * STRIP)
                lhs[0, strip, to, at] = high
                lhs[1, strip, to, at] = low

    def turn_cut(number, strips, pairs):
        some = slice(pairs[0] * STRIP, (pairs[-1] + 1) * STRIP)
        rows = len(strips) * len(pairs) * STRIP
        m, cut = number // 3, slice(number % 3 * 256, number % 3 * 256 + 256)
        way = m + 2 if m else 0
        wide = slice(m * WIDE, (m + 1) * WIDE)
        high = jnp.concatenate([lhs[0, s, some, wide] for s in strips])
        low = jnp.concatenate([lhs[1, s, some, wide] for s in strips])
        both = dot(jnp.concatenate([high, low]), w_high[way, :, cut])
        pots[m, :rows, cut] = both[:rows] + both[rows:] + dot(high, w_low[way, :, cut])

    def forward(*parts):
        products(*parts)
        for number in range(9):
            forward_cut(number, parts)

    def chain(parts, pairs, strips, turned):
        if parts:
            products(*parts)
        for step in range(14):
            if parts and step < 9:
                forward_cut(step, parts)
            if 0 <= step - 1 < 9:
                there_cut(step - 1, pairs)
            if 0 <= step - 2 < 9:
                back_cut(step - 2, pairs)
            if turned and step >= 5:
                turn_cut(step - 5, strips, turned)

    def weigh(number, side, strip, pairs, start, sums):
        at = slice(strip * STRIP, (strip + 1) * STRIP)
        for n in pairs:
            row = (number * len(pairs) + n - pairs[0]) * STRIP
            p, f, h = (
                [pots[m, row : row + STRIP, BLOCK * y + start : BLOCK * y + start + 128] for y in range(2)]
                for m in range(3)
            )
            f.append(-(f[0] + f[1]))
            h.append(h[1] - h[0])
            for y in range(6):
                value = p[y % 2] + f[y % 3]
                value = value + h[y] if y < 3 else value - h[y - 3]
                c = slice(BLOCK * y + start, BLOCK * y + start + 128)
                term = value * buf[n // 2, n % 2, side, at, c]
                sums[y] = term if sums[y] is None else sums[y] + term
        return sums

    def early():
        for number in range(2 * STRIPS):
            side, strip = divmod(number, STRIPS)
            for start in range(0, BLOCK, 128):
                sums = weigh(number, side, strip, (0, 1), start, [None] * 6)
                for y in range(6):
                    c = slice(BLOCK * y + start, BLOCK * y + start + 128)
                    acc[side, strip * STRIP : (strip + 1) * STRIP, c] = sums[y]

    def backward(side):
        if side == 0:
            for number in range(9):
                turn_cut(number, range(STRIPS), LATE)
        copies = []
        scale = 1.0 / root(grid)
        for strip in range(STRIPS):
            at = slice(strip * STRIP, (strip + 1) * STRIP)
            for start in range(0, BLOCK, 128):
                cols = [slice(BLOCK * y + start, BLOCK * y + start + 128) for y in range(6)]
                sums = weigh(strip, side, strip, LATE, start, [acc[side, at, c] for c in cols])
                for value, c in zip(sums, cols):
                    acc[side, at, c] = value * scale
            rows = pl.ds(strip * STRIP, STRIP)
            if side == 1:
                copies.append(
                    pltpu.make_async_remote_copy(
                        src_ref=acc.at[1, rows],
                        dst_ref=out.at[grid, rows],
                        send_sem=out_send.at[strip],
                        recv_sem=out_recv.at[strip],
                        device_id=across,
                        device_id_type=MESH,
                    )
                )
            else:
                copies.append(pltpu.make_async_copy(acc.at[0, rows], out.at[grid, rows], keep.at[strip]))
            copies[-1].start()
        return copies

    even = jnp.logical_not(odd)

    pl.semaphore_wait(barrier, 2)
    start(own)

    @pl.when(even)
    def _():
        start(swap)

    loads[1].wait()
    loads[2].wait()
    for m in range(5):
        build(m)

    @pl.when(even)
    def _():
        for k in range(2):
            own[k].wait_recv()
            own_on[k].start()

    for k in range(2):
        @pl.when(even)
        def _():
            swap[k].wait_recv()
            other[k].start()

        @pl.when(odd)
        def _():
            own[k].wait_recv()
            swap[k].start()
            own_on[k].start()

    for c in loads[3:]:
        c.wait()
    forward((0, 0), (1, 0))

    for k in range(2):
        @pl.when(odd)
        def _():
            swap[k].wait_recv()
            other[k].start()

        own_on[k].wait_recv()

        @pl.when(odd)
        def _():
            other_swap[k].start()

    forward((0, 1), (2, 0))

    def pass_on(k):
        @pl.when(odd)
        def _():
            other[k].wait_recv()
            other_on[k].start()

    pass_on(0)
    chain((), (0, 1), range(2 * STRIPS), (0, 1))
    early()
    pass_on(1)

    @pl.when(even)
    def _():
        arrived(other)

    arrived(other_on)
    chain(((1, 1), (2, 1)), LATE, range(STRIPS, 2 * STRIPS), LATE)
    sent = backward(1)
    kept = backward(0)
    for c in swap + own + own_on + other:
        c.wait_send()

    @pl.when(odd)
    def _():
        for c in other_on + other_swap:
            c.wait_send()

    for c in kept + sent:
        c.wait()


def per_device(orbitals, occupation):
    count, slab, plane = orbitals.shape
    operands = [orbitals] + [jnp.asarray(t) for t in tables()]
    return pl.pallas_call(
        kernel,
        out_shape=jax.ShapeDtypeStruct((count, slab, plane), jnp.float32),
        in_specs=[pl.BlockSpec(memory_space=pltpu.HBM)] * 7,
        out_specs=pl.BlockSpec(memory_space=pltpu.HBM),
        scratch_shapes=[pltpu.SMEM((count,), jnp.float32)]
        + [pltpu.VMEM(t.shape, t.dtype) for t in operands]
        + [
            pltpu.VMEM((3, count, 2, slab, plane), jnp.float32),
            pltpu.VMEM((5, WIDE, WIDE), jnp.bfloat16),
            pltpu.VMEM((5, WIDE, WIDE), jnp.bfloat16),
            pltpu.VMEM((3, 4 * N, WIDE), jnp.bfloat16),
            pltpu.VMEM((PAIRS, 2 * SIDE, plane), jnp.bfloat16),
            pltpu.VMEM((PAIRS, 3 * N, plane), jnp.bfloat16),
            pltpu.VMEM((2, 2 * STRIPS, PAIRS * STRIP, plane), jnp.bfloat16),
            pltpu.VMEM((3, 2 * ROWS // 3, WIDE), jnp.float32),
            pltpu.VMEM((2, slab, plane), jnp.float32),
            pltpu.SemaphoreType.DMA((7,)),
            pltpu.SemaphoreType.DMA((6, count)),
            pltpu.SemaphoreType.DMA((3, 2, count)),
            pltpu.SemaphoreType.DMA((STRIPS,)),
            pltpu.SemaphoreType.DMA((STRIPS,)),
            pltpu.SemaphoreType.DMA((STRIPS,)),
        ],
        compiler_params=pltpu.CompilerParams(
            vmem_limit_bytes=63 << 20, collective_id=0, has_side_effects=True
        ),
    )(occupation, *operands)


def solution(mesh):
    placed = (P("band", "grid", None), P("band"))
    return jax.shard_map(
        per_device, mesh=mesh, in_specs=placed, out_specs=P("band", "grid", None), check_vma=False
    )
```

```python
import jax
import jax.numpy as jnp
import numpy as np
from jax import lax
from jax.experimental import pallas as pl
from jax.experimental.pallas import tpu as pltpu
from jax.sharding import PartitionSpec as P

N = 48
HALF = N // 2
PLANE = N * N
BLOCK = 8 * N
WIDE = 2 * BLOCK
PAD = 8
SIDE = 3 * HALF + PAD
PAIRS = 6
ROWS = PAIRS * HALF
STRIP = 8
STRIPS = HALF // STRIP
LATE = (2, 3, 4, 5)
PLACE = (1, 0, 2)
MESH = pl.DeviceIdType.MESH


def cas(product, length):
    angle = (product % length) * (2.0 * np.pi / length)
    return np.cos(angle) + np.sin(angle)


def tables():
    i = np.arange(N)
    classes = [i[i % 3 == 0], i[(i % 6 == 2) | (i % 6 == 4)], i[(i % 6 == 1) | (i % 6 == 5)]]
    along_z = np.tile(cas(i[:, None] * i[None, :], N), (1, 16))
    ways = [cas(np.arange(16)[:, None] * k[None, :], N) for k in classes]
    along_y = np.stack([np.repeat(m, N, axis=1) for m in (*ways, ways[1].T, ways[2].T)])
    square = np.where(i <= HALF, i, i - N).astype(np.float64) ** 2
    order = np.concatenate(classes)
    total = square[:, None, None] + square[order][None, :, None] + square[None, None, :]
    coulomb = np.where(total > 0, 24.0 * 24.0 / np.pi / np.where(total > 0, total, 1.0), 0.0)
    coulomb = coulomb.reshape(N, PLANE) * (-0.25 / N**3)
    along_x = cas(i[:, None] * i[None, :], N)
    x_high = along_x.astype(np.float32).astype(jnp.bfloat16)
    x_low = (along_x - x_high.astype(np.float64)).astype(np.float32).astype(jnp.bfloat16)
    there, back = [], []
    for place in range(2):
        halves = [slice(s * HALF, (s + 1) * HALF) for s in (place, 1 - place)]
        pad = np.zeros((N, PAD), x_high.dtype)
        there.append(
            np.concatenate(
                [b for s in halves for b in (x_high[:, s], x_high[:, s], x_low[:, s], pad)], axis=1
            )
        )
        high, low = (np.concatenate([m[s] for s in halves]) for m in (x_high, x_low))
        back.append(np.concatenate([high, high, low], axis=1))
    return (
        along_z.astype(np.float32),
        along_y.astype(np.float32),
        np.stack(there),
        np.stack(back),
        coulomb.astype(np.float32),
    )


def split(value):
    high = value.astype(jnp.bfloat16)
    return high, (value - high.astype(jnp.float32)).astype(jnp.bfloat16)


def split32(value):
    high = value.astype(jnp.bfloat16).astype(jnp.float32)
    return high, value - high


def dot(a, b):
    return jnp.dot(a, b, preferred_element_type=jnp.float32)


def kernel(
    occ_in, psi_in, z_in, y_in, there_in, back_in, coulomb_in,
    out, occ, psi, along_z, along_y, there, back, coulomb,
    buf, w_high, w_low, slabs, xrhs, mid, lhs, pots, acc, load, send, recv, out_send, out_recv, keep,
):
    weights = pltpu.make_async_copy(occ_in, occ, load.at[6])
    weights.start()
    sources = (psi_in, z_in, y_in, there_in, back_in, coulomb_in)
    targets = (psi, along_z, along_y, there, back, coulomb)
    loads = [pltpu.make_async_copy(a, b, load.at[i]) for i, (a, b) in enumerate(zip(sources, targets))]
    for c in loads:
        c.start()
    band, grid = lax.axis_index("band"), lax.axis_index("grid")
    devices = lax.axis_size("band")
    left = {"band": lax.rem(band + devices - 1, devices), "grid": grid}
    right = {"band": lax.rem(band + 1, devices), "grid": grid}
    across = {"band": band, "grid": 1 - grid}
    odd = lax.rem(band, 2) == 1

    barrier = pltpu.get_barrier_semaphore()
    for device in (across, right):
        pl.semaphore_signal(barrier, inc=1, device_id=device, device_id_type=MESH)

    def root(k):
        return jnp.sqrt(jnp.full((1, 128), occ[k], jnp.float32))

    weights.wait()
    loads[0].wait()
    for k in range(2):
        factor = root(k)
        for start in range(0, PLANE, 128):
            at = slice(start, start + 128)
            buf[0, k, 0, :, at] = psi[k, :, at] * factor

    def copy(number, k, source, target, device):
        return pltpu.make_async_remote_copy(
            src_ref=buf.at[source[0], k, source[1]],
            dst_ref=buf.at[target[0], k, target[1]],
            send_sem=send.at[number, k],
            recv_sem=recv.at[target[0], target[1], k],
            device_id=device,
            device_id_type=MESH,
        )

    swap = [copy(0, k, (0, 0), (0, 1), across) for k in (1 - grid, grid)]
    own = [copy(1, k, (0, 0), (1, 0), left) for k in range(2)]
    own_on = [copy(2, k, (1, 0), (2, 0), left) for k in range(2)]
    other = [copy(3, k, (0, 1), (1, 1), left) for k in range(2)]
    other_on = [copy(4, k, (1, 1), (2, 1), left) for k in range(2)]
    next_swap = [copy(5, k, (1, 0), (1, 1), across) for k in range(2)]
    swapped = [copy(0, k, (0, 0), (0, 1), across) for k in range(2)]

    def start(copies):
        for c in copies:
            c.start()

    def arrived(copies):
        for c in copies:
            c.wait_recv()

    def build(m):
        @pl.loop(0, 16)
        def _(y):
            rows = pl.ds(pl.multiple_of(y * N, 16), N)
            high, low = split(along_z[...] * along_y[m, pl.ds(y, 1), :])
            w_high[m, rows, :] = high
            w_low[m, rows, :] = low

    def products(*parts):
        rows = N * len(parts)
        for start in range(0, BLOCK, 128):
            cols = [slice(BLOCK * y + start, BLOCK * y + start + 128) for y in range(6)]
            for n, (stop, side) in enumerate(parts):
                to_rows = slice(n * N, (n + 1) * N)
                lows = slice(rows + n * N, rows + (n + 1) * N)
                a = [
                    jnp.concatenate([buf[0, grid, side, :, c] * buf[stop, k, side, :, c] for k in range(2)])
                    for c in cols
                ]
                plus = [a[y] + a[y + 3] for y in range(3)]
                minus = [a[y] - a[y + 3] for y in range(3)]
                sums = (
                    (a[0] + a[2] + a[4], a[1] + a[3] + a[5]),
                    (plus[0] - plus[2], plus[1] - plus[2]),
                    (minus[0] - minus[2], minus[1] + minus[2]),
                )
                for m, pair in enumerate(sums):
                    for y, value in enumerate(pair):
                        to = slice(y * BLOCK + start, y * BLOCK + start + 128)
                        slabs[m, to_rows, to], slabs[m, lows, to] = split(value)
    def forward_cut(number, parts):
        rows = N * len(parts)
        pad = jnp.zeros((PAD, 256), jnp.float32)
        m, cut = number // 3, slice(number % 3 * 256, number % 3 * 256 + 256)
        both = dot(slabs[m, : 2 * rows], w_high[m, :, cut])
        value = both[:rows] + both[rows:] + dot(slabs[m, :rows, :], w_low[m, :, cut])
        high, low = split32(value)
        to = slice(number * 256, number * 256 + 256)
        for n, (stop, side) in enumerate(parts):
            for k in range(2):
                at = slice((2 * n + k) * HALF, (2 * n + k + 1) * HALF)
                block = jnp.concatenate([high[at], low[at], high[at], pad])
                xrhs[2 * PLACE[stop] + k, side * SIDE : (side + 1) * SIDE, to] = block.astype(jnp.bfloat16)

    def there_cut(number, pairs):
        at = slice(number * 256, number * 256 + 256)
        for n in pairs:
            high, low = split(dot(there[grid], xrhs[n, :, at]) * coulomb[:, at])
            mid[n, :, at] = jnp.concatenate([high, low, high])

    def back_cut(number, pairs):
        at = slice(number * 256, number * 256 + 256)
        for n in pairs[::2]:
            one, two = dot(back[grid], mid[n, :, at]), dot(back[grid], mid[n + 1, :, at])
            for strip in range(2 * STRIPS):
                rows = slice(strip * STRIP, (strip + 1) * STRIP)
                high, low = split(jnp.concatenate([one[rows], two[rows]]))
                to = slice(n * STRIP, (n + 2) * STRIP)
                lhs[0, strip, to, at] = high
                lhs[1, strip, to, at] = low

    def turn_cut(number, strips, pairs):
        some = slice(pairs[0] * STRIP, (pairs[-1] + 1) * STRIP)
        rows = len(strips) * len(pairs) * STRIP
        m, cut = number // 3, slice(number % 3 * 256, number % 3 * 256 + 256)
        way = m + 2 if m else 0
        wide = slice(m * WIDE, (m + 1) * WIDE)
        high = jnp.concatenate([lhs[0, s, some, wide] for s in strips])
        low = jnp.concatenate([lhs[1, s, some, wide] for s in strips])
        both = dot(jnp.concatenate([high, low]), w_high[way, :, cut])
        pots[m, :rows, cut] = both[:rows] + both[rows:] + dot(high, w_low[way, :, cut])

    def forward(*parts):
        products(*parts)
        for number in range(9):
            forward_cut(number, parts)

    def chain(parts, pairs, strips, turned):
        if parts:
            products(*parts)
        for step in range(14):
            if parts and step < 9:
                forward_cut(step, parts)
            if 0 <= step - 1 < 9:
                there_cut(step - 1, pairs)
            if 0 <= step - 2 < 9:
                back_cut(step - 2, pairs)
            if turned and step >= 5:
                turn_cut(step - 5, strips, turned)

    def weigh(number, side, strip, pairs, start, sums):
        at = slice(strip * STRIP, (strip + 1) * STRIP)
        for n in pairs:
            row = (number * len(pairs) + n - pairs[0]) * STRIP
            p, f, h = (
                [pots[m, row : row + STRIP, BLOCK * y + start : BLOCK * y + start + 128] for y in range(2)]
                for m in range(3)
            )
            f.append(-(f[0] + f[1]))
            h.append(h[1] - h[0])
            for y in range(6):
                value = p[y % 2] + f[y % 3]
                value = value + h[y] if y < 3 else value - h[y - 3]
                c = slice(BLOCK * y + start, BLOCK * y + start + 128)
                term = value * buf[PLACE[n // 2], n % 2, side, at, c]
                sums[y] = term if sums[y] is None else sums[y] + term
        return sums

    def early():
        for number in range(2 * STRIPS):
            side, strip = divmod(number, STRIPS)
            for start in range(0, BLOCK, 128):
                sums = weigh(number, side, strip, (0, 1), start, [None] * 6)
                for y in range(6):
                    c = slice(BLOCK * y + start, BLOCK * y + start + 128)
                    acc[side, strip * STRIP : (strip + 1) * STRIP, c] = sums[y]

    def backward(side):
        if side == 0:
            for number in range(9):
                turn_cut(number, range(STRIPS), LATE)
        copies = []
        scale = 1.0 / root(grid)
        for strip in range(STRIPS):
            at = slice(strip * STRIP, (strip + 1) * STRIP)
            for start in range(0, BLOCK, 128):
                cols = [slice(BLOCK * y + start, BLOCK * y + start + 128) for y in range(6)]
                sums = weigh(strip, side, strip, LATE, start, [acc[side, at, c] for c in cols])
                for value, c in zip(sums, cols):
                    acc[side, at, c] = value * scale
            rows = pl.ds(strip * STRIP, STRIP)
            if side == 1:
                copies.append(
                    pltpu.make_async_remote_copy(
                        src_ref=acc.at[1, rows],
                        dst_ref=out.at[grid, rows],
                        send_sem=out_send.at[strip],
                        recv_sem=out_recv.at[strip],
                        device_id=across,
                        device_id_type=MESH,
                    )
                )
            else:
                copies.append(pltpu.make_async_copy(acc.at[0, rows], out.at[grid, rows], keep.at[strip]))
            copies[-1].start()
        return copies

    even = jnp.logical_not(odd)

    pl.semaphore_wait(barrier, 2)
    start(own)

    @pl.when(odd)
    def _():
        start(swap)

    loads[1].wait()
    loads[2].wait()
    for m in range(5):
        build(m)

    @pl.when(even)
    def _():
        for k in range(2):
            own[k].wait_recv()
            own_on[k].start()
        swap[0].start()
        for k in range(2):
            other[k].wait_recv()
            other_on[k].start()
            if k == 1:
                swap[1].start()

    @pl.when(odd)
    def _():
        for k in range(2):
            own[k].wait_recv()
            own_on[k].start()
            next_swap[k].start()
            swapped[k].wait_recv()
            other[k].start()

    for c in loads[3:]:
        c.wait()
    forward((0, 0), (1, 0))

    @pl.when(odd)
    def _():
        for k in range(2):
            next_swap[k].wait_recv()
            other_on[k].start()

    @pl.when(even)
    def _():
        swap[1].wait_recv()

    arrived(own_on)
    forward((1, 1), (2, 0))
    chain((), (0, 1), range(2 * STRIPS), (0, 1))
    early()

    @pl.when(even)
    def _():
        arrived(other_on)
        swap[0].wait_recv()

    @pl.when(odd)
    def _():
        arrived(other_on)

    chain(((0, 1), (2, 1)), LATE, range(STRIPS, 2 * STRIPS), LATE)
    sent = backward(1)
    kept = backward(0)
    for c in swap + own + own_on + other_on:
        c.wait_send()

    @pl.when(odd)
    def _():
        for c in other + next_swap:
            c.wait_send()

    for c in kept + sent:
        c.wait()


def per_device(orbitals, occupation):
    count, slab, plane = orbitals.shape
    operands = [orbitals] + [jnp.asarray(t) for t in tables()]
    return pl.pallas_call(
        kernel,
        out_shape=jax.ShapeDtypeStruct((count, slab, plane), jnp.float32),
        in_specs=[pl.BlockSpec(memory_space=pltpu.HBM)] * 7,
        out_specs=pl.BlockSpec(memory_space=pltpu.HBM),
        scratch_shapes=[pltpu.SMEM((count,), jnp.float32)]
        + [pltpu.VMEM(t.shape, t.dtype) for t in operands]
        + [
            pltpu.VMEM((3, count, 2, slab, plane), jnp.float32),
            pltpu.VMEM((5, WIDE, WIDE), jnp.bfloat16),
            pltpu.VMEM((5, WIDE, WIDE), jnp.bfloat16),
            pltpu.VMEM((3, 4 * N, WIDE), jnp.bfloat16),
            pltpu.VMEM((PAIRS, 2 * SIDE, plane), jnp.bfloat16),
            pltpu.VMEM((PAIRS, 3 * N, plane), jnp.bfloat16),
            pltpu.VMEM((2, 2 * STRIPS, PAIRS * STRIP, plane), jnp.bfloat16),
            pltpu.VMEM((3, 2 * ROWS // 3, WIDE), jnp.float32),
            pltpu.VMEM((2, slab, plane), jnp.float32),
            pltpu.SemaphoreType.DMA((7,)),
            pltpu.SemaphoreType.DMA((6, count)),
            pltpu.SemaphoreType.DMA((3, 2, count)),
            pltpu.SemaphoreType.DMA((STRIPS,)),
            pltpu.SemaphoreType.DMA((STRIPS,)),
            pltpu.SemaphoreType.DMA((STRIPS,)),
        ],
        compiler_params=pltpu.CompilerParams(
            vmem_limit_bytes=63 << 20, collective_id=0, has_side_effects=True
        ),
    )(occupation, *operands)


def solution(mesh):
    placed = (P("band", "grid", None), P("band"))
    return jax.shard_map(
        per_device, mesh=mesh, in_specs=placed, out_specs=P("band", "grid", None), check_vma=False
    )
```

```python
import jax
import jax.numpy as jnp
import numpy as np
from jax import lax
from jax.experimental import pallas as pl
from jax.experimental.pallas import tpu as pltpu
from jax.sharding import PartitionSpec as P

N = 48
HALF = N // 2
PLANE = N * N
BLOCK = 8 * N
WIDE = 2 * BLOCK
PAD = 8
SIDE = 3 * HALF + PAD
PAIRS = 6
ROWS = PAIRS * HALF
STRIP = 8
STRIPS = HALF // STRIP
LATE = (2, 3, 4, 5)
PLACE = (1, 0, 2)
MESH = pl.DeviceIdType.MESH


def cas(product, length):
    angle = (product % length) * (2.0 * np.pi / length)
    return np.cos(angle) + np.sin(angle)


def tables():
    i = np.arange(N)
    classes = [i[i % 3 == 0], i[(i % 6 == 2) | (i % 6 == 4)], i[(i % 6 == 1) | (i % 6 == 5)]]
    along_z = np.tile(cas(i[:, None] * i[None, :], N), (1, 16))
    ways = [cas(np.arange(16)[:, None] * k[None, :], N) for k in classes]
    along_y = np.stack([np.repeat(m, N, axis=1) for m in (*ways, ways[1].T, ways[2].T)])
    square = np.where(i <= HALF, i, i - N).astype(np.float64) ** 2
    order = np.concatenate(classes)
    total = square[:, None, None] + square[order][None, :, None] + square[None, None, :]
    coulomb = np.where(total > 0, 24.0 * 24.0 / np.pi / np.where(total > 0, total, 1.0), 0.0)
    coulomb = coulomb.reshape(N, PLANE) * (-0.25 / N**3)
    along_x = cas(i[:, None] * i[None, :], N)
    x_high = along_x.astype(np.float32).astype(jnp.bfloat16)
    x_low = (along_x - x_high.astype(np.float64)).astype(np.float32).astype(jnp.bfloat16)
    there, back = [], []
    for place in range(2):
        halves = [slice(s * HALF, (s + 1) * HALF) for s in (place, 1 - place)]
        pad = np.zeros((N, PAD), x_high.dtype)
        there.append(
            np.concatenate(
                [b for s in halves for b in (x_high[:, s], x_high[:, s], x_low[:, s], pad)], axis=1
            )
        )
        high, low = (np.concatenate([m[s] for s in halves]) for m in (x_high, x_low))
        back.append(np.concatenate([high, high, low], axis=1))
    return (
        along_z.astype(np.float32),
        along_y.astype(np.float32),
        np.stack(there),
        np.stack(back),
        coulomb.astype(np.float32),
    )


def split(value):
    high = value.astype(jnp.bfloat16)
    return high, (value - high.astype(jnp.float32)).astype(jnp.bfloat16)


def split32(value):
    high = value.astype(jnp.bfloat16).astype(jnp.float32)
    return high, value - high


def dot(a, b):
    return jnp.dot(a, b, preferred_element_type=jnp.float32)


def kernel(
    occ_in, psi_in, z_in, y_in, there_in, back_in, coulomb_in,
    out, occ, psi, along_z, along_y, there, back, coulomb,
    buf, w_high, w_low, slabs, xrhs, mid, lhs, pots, acc, load, send, recv, out_send, out_recv, keep,
):
    weights = pltpu.make_async_copy(occ_in, occ, load.at[6])
    weights.start()
    sources = (psi_in, z_in, y_in, there_in, back_in, coulomb_in)
    targets = (psi, along_z, along_y, there, back, coulomb)
    loads = [pltpu.make_async_copy(a, b, load.at[i]) for i, (a, b) in enumerate(zip(sources, targets))]
    loads[0].start()
    band, grid = lax.axis_index("band"), lax.axis_index("grid")
    devices = lax.axis_size("band")
    left = {"band": lax.rem(band + devices - 1, devices), "grid": grid}
    right = {"band": lax.rem(band + 1, devices), "grid": grid}
    across = {"band": band, "grid": 1 - grid}
    odd = lax.rem(band, 2) == 1

    barrier = pltpu.get_barrier_semaphore()
    for device in (across, right):
        pl.semaphore_signal(barrier, inc=1, device_id=device, device_id_type=MESH)

    def root(k):
        return jnp.sqrt(jnp.full((1, 128), occ[k], jnp.float32))

    weights.wait()
    loads[0].wait()
    for k in range(2):
        factor = root(k)
        for start in range(0, PLANE, 128):
            at = slice(start, start + 128)
            buf[0, k, 0, :, at] = psi[k, :, at] * factor

    def copy(number, k, source, target, device):
        return pltpu.make_async_remote_copy(
            src_ref=buf.at[source[0], k, source[1]],
            dst_ref=buf.at[target[0], k, target[1]],
            send_sem=send.at[number, k],
            recv_sem=recv.at[target[0], target[1], k],
            device_id=device,
            device_id_type=MESH,
        )

    swap = [copy(0, k, (0, 0), (0, 1), across) for k in (1 - grid, grid)]
    own = [copy(1, k, (0, 0), (1, 0), left) for k in range(2)]
    own_on = [copy(2, k, (1, 0), (2, 0), left) for k in range(2)]
    other = [copy(3, k, (0, 1), (1, 1), left) for k in range(2)]
    other_on = [copy(4, k, (1, 1), (2, 1), left) for k in range(2)]
    next_swap = [copy(5, k, (1, 0), (1, 1), across) for k in range(2)]
    swapped = [copy(0, k, (0, 0), (0, 1), across) for k in range(2)]

    def start(copies):
        for c in copies:
            c.start()

    def arrived(copies):
        for c in copies:
            c.wait_recv()

    def build(m):
        @pl.loop(0, 16)
        def _(y):
            rows = pl.ds(pl.multiple_of(y * N, 16), N)
            high, low = split(along_z[...] * along_y[m, pl.ds(y, 1), :])
            w_high[m, rows, :] = high
            w_low[m, rows, :] = low

    def products(*parts):
        rows = N * len(parts)
        for start in range(0, BLOCK, 128):
            cols = [slice(BLOCK * y + start, BLOCK * y + start + 128) for y in range(6)]
            for n, (stop, side) in enumerate(parts):
                to_rows = slice(n * N, (n + 1) * N)
                lows = slice(rows + n * N, rows + (n + 1) * N)
                a = [
                    jnp.concatenate([buf[0, grid, side, :, c] * buf[stop, k, side, :, c] for k in range(2)])
                    for c in cols
                ]
                plus = [a[y] + a[y + 3] for y in range(3)]
                minus = [a[y] - a[y + 3] for y in range(3)]
                sums = (
                    (a[0] + a[2] + a[4], a[1] + a[3] + a[5]),
                    (plus[0] - plus[2], plus[1] - plus[2]),
                    (minus[0] - minus[2], minus[1] + minus[2]),
                )
                for m, pair in enumerate(sums):
                    for y, value in enumerate(pair):
                        to = slice(y * BLOCK + start, y * BLOCK + start + 128)
                        slabs[m, to_rows, to], slabs[m, lows, to] = split(value)
    def forward_cut(number, parts):
        rows = N * len(parts)
        pad = jnp.zeros((PAD, 256), jnp.float32)
        m, cut = number // 3, slice(number % 3 * 256, number % 3 * 256 + 256)
        both = dot(slabs[m, : 2 * rows], w_high[m, :, cut])
        value = both[:rows] + both[rows:] + dot(slabs[m, :rows, :], w_low[m, :, cut])
        high, low = split32(value)
        to = slice(number * 256, number * 256 + 256)
        for n, (stop, side) in enumerate(parts):
            for k in range(2):
                at = slice((2 * n + k) * HALF, (2 * n + k + 1) * HALF)
                block = jnp.concatenate([high[at], low[at], high[at], pad])
                xrhs[2 * PLACE[stop] + k, side * SIDE : (side + 1) * SIDE, to] = block.astype(jnp.bfloat16)

    def there_cut(number, pairs):
        at = slice(number * 256, number * 256 + 256)
        for n in pairs:
            high, low = split(dot(there[grid], xrhs[n, :, at]) * coulomb[:, at])
            mid[n, :, at] = jnp.concatenate([high, low, high])

    def back_cut(number, pairs):
        at = slice(number * 256, number * 256 + 256)
        for n in pairs[::2]:
            one, two = dot(back[grid], mid[n, :, at]), dot(back[grid], mid[n + 1, :, at])
            for strip in range(2 * STRIPS):
                rows = slice(strip * STRIP, (strip + 1) * STRIP)
                high, low = split(jnp.concatenate([one[rows], two[rows]]))
                to = slice(n * STRIP, (n + 2) * STRIP)
                lhs[0, strip, to, at] = high
                lhs[1, strip, to, at] = low

    def turn_cut(number, strips, pairs):
        some = slice(pairs[0] * STRIP, (pairs[-1] + 1) * STRIP)
        rows = len(strips) * len(pairs) * STRIP
        m, cut = number // 3, slice(number % 3 * 256, number % 3 * 256 + 256)
        way = m + 2 if m else 0
        wide = slice(m * WIDE, (m + 1) * WIDE)
        high = jnp.concatenate([lhs[0, s, some, wide] for s in strips])
        low = jnp.concatenate([lhs[1, s, some, wide] for s in strips])
        both = dot(jnp.concatenate([high, low]), w_high[way, :, cut])
        pots[m, :rows, cut] = both[:rows] + both[rows:] + dot(high, w_low[way, :, cut])

    def forward(*parts):
        products(*parts)
        for number in range(9):
            forward_cut(number, parts)

    def chain(parts, pairs, strips, turned):
        if parts:
            products(*parts)
        for step in range(14):
            if parts and step < 9:
                forward_cut(step, parts)
            if 0 <= step - 1 < 9:
                there_cut(step - 1, pairs)
            if 0 <= step - 2 < 9:
                back_cut(step - 2, pairs)
            if turned and step >= 5:
                turn_cut(step - 5, strips, turned)

    def weigh(number, side, strip, pairs, start, sums):
        at = slice(strip * STRIP, (strip + 1) * STRIP)
        for n in pairs:
            row = (number * len(pairs) + n - pairs[0]) * STRIP
            p, f, h = (
                [pots[m, row : row + STRIP, BLOCK * y + start : BLOCK * y + start + 128] for y in range(2)]
                for m in range(3)
            )
            f.append(-(f[0] + f[1]))
            h.append(h[1] - h[0])
            for y in range(6):
                value = p[y % 2] + f[y % 3]
                value = value + h[y] if y < 3 else value - h[y - 3]
                c = slice(BLOCK * y + start, BLOCK * y + start + 128)
                term = value * buf[PLACE[n // 2], n % 2, side, at, c]
                sums[y] = term if sums[y] is None else sums[y] + term
        return sums

    def early():
        for number in range(2 * STRIPS):
            side, strip = divmod(number, STRIPS)
            for start in range(0, BLOCK, 128):
                sums = weigh(number, side, strip, (0, 1), start, [None] * 6)
                for y in range(6):
                    c = slice(BLOCK * y + start, BLOCK * y + start + 128)
                    acc[side, strip * STRIP : (strip + 1) * STRIP, c] = sums[y]

    def backward(side):
        if side == 0:
            for number in range(9):
                turn_cut(number, range(STRIPS), LATE)
        copies = []
        scale = 1.0 / root(grid)
        for strip in range(STRIPS):
            at = slice(strip * STRIP, (strip + 1) * STRIP)
            for start in range(0, BLOCK, 128):
                cols = [slice(BLOCK * y + start, BLOCK * y + start + 128) for y in range(6)]
                sums = weigh(strip, side, strip, LATE, start, [acc[side, at, c] for c in cols])
                for value, c in zip(sums, cols):
                    acc[side, at, c] = value * scale
            rows = pl.ds(strip * STRIP, STRIP)
            if side == 1:
                copies.append(
                    pltpu.make_async_remote_copy(
                        src_ref=acc.at[1, rows],
                        dst_ref=out.at[grid, rows],
                        send_sem=out_send.at[strip],
                        recv_sem=out_recv.at[strip],
                        device_id=across,
                        device_id_type=MESH,
                    )
                )
            else:
                copies.append(pltpu.make_async_copy(acc.at[0, rows], out.at[grid, rows], keep.at[strip]))
            copies[-1].start()
        return copies

    even = jnp.logical_not(odd)

    for c in loads[1:]:
        c.start()
    pl.semaphore_wait(barrier, 2)
    start(own)

    @pl.when(odd)
    def _():
        start(swapped)

    loads[1].wait()
    loads[2].wait()
    for m in range(5):
        build(m)

    @pl.when(even)
    def _():
        for k in range(2):
            own[k].wait_recv()
            own_on[k].start()
        swap[0].start()
        for k in range(2):
            other[k].wait_recv()
            other_on[k].start()
            if k == 1:
                swap[1].start()

    @pl.when(odd)
    def _():
        for k in range(2):
            own[k].wait_recv()
            own_on[k].start()
            next_swap[k].start()
            swapped[k].wait_recv()
            other[k].start()

    for c in loads[3:]:
        c.wait()
    forward((0, 0), (1, 0))

    @pl.when(odd)
    def _():
        for k in range(2):
            next_swap[k].wait_recv()
            other_on[k].start()

    @pl.when(even)
    def _():
        swap[1].wait_recv()

    arrived(own_on)
    forward((1, 1), (2, 0))
    chain((), (0, 1), range(2 * STRIPS), (0, 1))
    early()

    @pl.when(even)
    def _():
        arrived(other_on)
        swap[0].wait_recv()

    @pl.when(odd)
    def _():
        arrived(other_on)

    chain(((0, 1), (2, 1)), LATE, range(STRIPS, 2 * STRIPS), LATE)
    sent = backward(1)
    kept = backward(0)
    for c in swap + own + own_on + other_on:
        c.wait_send()

    @pl.when(odd)
    def _():
        for c in other + next_swap:
            c.wait_send()

    for c in kept + sent:
        c.wait()


def per_device(orbitals, occupation):
    count, slab, plane = orbitals.shape
    operands = [orbitals] + [jnp.asarray(t) for t in tables()]
    return pl.pallas_call(
        kernel,
        out_shape=jax.ShapeDtypeStruct((count, slab, plane), jnp.float32),
        in_specs=[pl.BlockSpec(memory_space=pltpu.HBM)] * 7,
        out_specs=pl.BlockSpec(memory_space=pltpu.HBM),
        scratch_shapes=[pltpu.SMEM((count,), jnp.float32)]
        + [pltpu.VMEM(t.shape, t.dtype) for t in operands]
        + [
            pltpu.VMEM((3, count, 2, slab, plane), jnp.float32),
            pltpu.VMEM((5, WIDE, WIDE), jnp.bfloat16),
            pltpu.VMEM((5, WIDE, WIDE), jnp.bfloat16),
            pltpu.VMEM((3, 4 * N, WIDE), jnp.bfloat16),
            pltpu.VMEM((PAIRS, 2 * SIDE, plane), jnp.bfloat16),
            pltpu.VMEM((PAIRS, 3 * N, plane), jnp.bfloat16),
            pltpu.VMEM((2, 2 * STRIPS, PAIRS * STRIP, plane), jnp.bfloat16),
            pltpu.VMEM((3, 2 * ROWS // 3, WIDE), jnp.float32),
            pltpu.VMEM((2, slab, plane), jnp.float32),
            pltpu.SemaphoreType.DMA((7,)),
            pltpu.SemaphoreType.DMA((6, count)),
            pltpu.SemaphoreType.DMA((3, 2, count)),
            pltpu.SemaphoreType.DMA((STRIPS,)),
            pltpu.SemaphoreType.DMA((STRIPS,)),
            pltpu.SemaphoreType.DMA((STRIPS,)),
        ],
        compiler_params=pltpu.CompilerParams(
            vmem_limit_bytes=63 << 20, collective_id=0, has_side_effects=True
        ),
    )(occupation, *operands)


def solution(mesh):
    placed = (P("band", "grid", None), P("band"))
    return jax.shard_map(
        per_device, mesh=mesh, in_specs=placed, out_specs=P("band", "grid", None), check_vma=False
    )
```
